128 devices in a mesh: tok: 16 (over x, y), head: 8 (over z, core).
Axes of the slice: x: 4, y: 4, z: 4, core: 2. Of those that a mesh axis runs over, the one named last changes fastest.
Arguments:
- new_qkv: bfloat16 [128, 512, 6144], P(('tok', 'head')), may hold values from -4.5 to 4.5, as said below
- kv_cache: bfloat16 [128, 512, 2048], P('tok', None, 'head'), may hold values from -4.5 to 4.5, as said below
- lengths: int32 [128], replicated, may hold values from 1 to 512, 32768 in all
- slot_of: int32 [128], replicated, may hold values from 0 to 127, as said below
Outputs:
- context: bfloat16 [128, 512, 4096], P(('tok', 'head'))
- appended: bfloat16 [128, 512, 2048], P('tok', None, 'head')
The draws below stay inside these ranges and needn't reach their ends.
Inputs may be any that keep to these rules, and one draw needn't show every extreme that they name: `new_qkv`: entries of the new tokens' queries, keys and values. `kv_cache`: entries of the cached keys and values; only the first lengths[r] positions of slot slot_of[r] are read. `slot_of`: a permutation of the slots; call the requests r with r // 8 = t, and the slots s with s // 8 = t, row t: the requests of one row have slots in different rows, and the slots of one row belong to requests of different rows.
All inputs are finite; a program needn't handle non-finite values.
Results may differ from the reference program's by a relative error of at most 0.0045.
Values may be sent and summed in bfloat16 or wider, within the bound.
A program may use at most 128 MiB of HBM per device.

```python
import math
import jax
import jax.numpy as jnp
import numpy as np
from jax import lax

QH = 32
KVH = 8
HD = 128
NEW = 512
CACHE = 512
REQ = 128
SLOT_DEV = 8
GROUP = 768


def draw_new_qkv(key, part):
    own_key = jax.random.fold_in(key, 11)
    drawn = jnp.clip(jax.random.normal(own_key, (REQ, NEW, KVH, GROUP), jnp.float32), -4.5, 4.5)
    return drawn.reshape(REQ, NEW, KVH * GROUP).astype(jnp.bfloat16)


def draw_kv_cache(key, part):
    own_key = jax.random.fold_in(key, 13)
    drawn = jnp.clip(jax.random.normal(own_key, (REQ, CACHE, KVH, 2, HD), jnp.float32), -4.5, 4.5)
    return drawn.reshape(REQ, CACHE, KVH * 2 * HD).astype(jnp.bfloat16)


def draw_slot_of(key, part):
    row_count = REQ // SLOT_DEV
    offsets = jax.random.permutation(jax.random.fold_in(key, 21), row_count)[:SLOT_DEV]
    row_order = jax.random.permutation(jax.random.fold_in(key, 22), row_count)
    within = jax.random.permutation(jax.random.fold_in(key, 23), SLOT_DEV)
    row_keys = jax.random.split(jax.random.fold_in(key, 24), row_count)
    shuffled = jax.vmap(lambda one_key: jax.random.permutation(one_key, SLOT_DEV))(row_keys).reshape(REQ)
    source_row = jnp.arange(REQ, dtype=jnp.int32) // SLOT_DEV
    target_row = row_order[(source_row + offsets[shuffled]) % row_count]
    return (target_row * SLOT_DEV + within[shuffled]).astype(jnp.int32)


def profile(count, total, reach, slope):
    loads = [(1 << 20) // math.isqrt(grade ** slope) + 1 for grade in range(2, count + 1)]
    spare, given = total - reach - (count - 1), [1] * (count - 1)
    while spare > 0:
        free = [i for i in range(count - 1) if given[i] < reach]
        whole, left = sum([loads[i] for i in free]), spare
        for i in free:
            more = min(reach - given[i], max(1, left * loads[i] // whole), spare)
            given[i] = given[i] + more
            spare = spare - more
    return np.array([reach] + given)


def uneven(rng, count, total, reach, slope):
    if count == 2:
        one = jax.random.randint(rng, (), max(1, total - reach), min(reach, total - 1) + 1)
        return jnp.stack([one, total - one])
    sizes = jnp.asarray(profile(count, total, reach, slope), jnp.int32)
    twos = (count - 1) // 2
    source_of, taker = sizes[1:1 + 2 * twos:2], sizes[2:2 + 2 * twos:2]
    slack = jnp.minimum(source_of - 1, reach - taker)
    moved = jax.random.randint(jax.random.fold_in(rng, 1), (twos,), 0, 1 << 20) % (slack + 1)
    sizes = sizes.at[1:1 + 2 * twos:2].set(source_of - moved).at[2:2 + 2 * twos:2].set(taker + moved)
    return sizes[jax.random.permutation(jax.random.fold_in(rng, 2), count)]


def setup_inputs(seed: int = 0) -> dict:
    seeds = jax.random.split(jax.random.key(seed), 5)
    return {
        "new_qkv": draw_new_qkv(jax.random.fold_in(seeds[4], 71), 0),
        "kv_cache": draw_kv_cache(jax.random.fold_in(seeds[4], 71), 0),
        "lengths": uneven(seeds[2], REQ, REQ * CACHE // 2, CACHE, 2).astype(jnp.int32),
        "slot_of": draw_slot_of(jax.random.fold_in(seeds[4], 71), 0),
    }


masked_score = -1e+30

def reference(new_qkv, kv_cache, lengths, slot_of):
    per_group = QH // KVH
    score_scale = 1.0 / math.sqrt(HD)
    request_of = jnp.argsort(slot_of).astype(jnp.int32)
    grouped = new_qkv.reshape(REQ, NEW, KVH, GROUP)
    appended = jnp.take(grouped, request_of, axis=0)[:, :, :, per_group * HD:].reshape(REQ, NEW, KVH * 2 * HD)

    def attend_one(request):
        new_rows = lax.dynamic_index_in_dim(grouped, request, 0, keepdims=False)
        cached = lax.dynamic_index_in_dim(kv_cache, slot_of[request], 0, keepdims=False).reshape(CACHE, KVH, 2, HD)
        length = lengths[request]
        queries = new_rows[:, :, :per_group * HD].reshape(NEW, KVH, per_group, HD).astype(jnp.float32)
        key_rows = jnp.concatenate([cached[:, :, 0], new_rows[:, :, per_group * HD:(per_group + 1) * HD]], 0).astype(jnp.float32)
        value_rows = jnp.concatenate([cached[:, :, 1], new_rows[:, :, (per_group + 1) * HD:]], 0).astype(jnp.float32)
        scores = jnp.einsum('qgha,kga->ghqk', queries, key_rows) * score_scale
        positions = jnp.arange(CACHE + NEW, dtype=jnp.int32)[None, :]
        query_pos = jnp.arange(NEW, dtype=jnp.int32)[:, None]
        visible = jnp.where(positions < CACHE, positions < length, positions - CACHE <= query_pos)
        scores = jnp.where(visible, scores, masked_score)
        row_max = lax.optimization_barrier(jnp.max(scores, -1, keepdims=True))
        weights = jnp.where(visible, jnp.exp(scores - row_max), 0.0)
        weight_sum = lax.optimization_barrier(jnp.sum(weights, -1))
        rounded = lax.optimization_barrier(weights.astype(jnp.bfloat16)).astype(jnp.float32)
        context = jnp.einsum('ghqk,kga->qgha', rounded, value_rows)
        context = context / jnp.transpose(weight_sum, (2, 0, 1))[..., None]
        return context.reshape(NEW, QH * HD).astype(jnp.bfloat16)
    context = lax.map(attend_one, jnp.arange(REQ, dtype=jnp.int32))
    return (context, appended)
```

```python
import functools
import math

import jax
import jax.numpy as jnp
from jax import lax
from jax.experimental import pallas as pl
from jax.experimental.pallas import tpu as pltpu
from jax.sharding import PartitionSpec as P

QH = 32
KVH = 8
HD = 128
NEW = 512
CACHE = 512
GROUP = 768
PER = QH // KVH
TQ = 256
MESH = pl.DeviceIdType.MESH

masked_score = -1e30


def head_attention(q_of, new_kv, cached_kv, bias, diagonal, write):
    factor = math.log2(math.e) / math.sqrt(HD)
    dims = (((1,), (1,)), ((), ()))
    for head in range(PER):
        for tile in range(NEW // TQ):
            first = tile * TQ
            q = q_of(head, first)
            old = lax.dot_general(
                q, cached_kv(0, CACHE, 0), dims, preferred_element_type=jnp.float32
            )
            old = old + bias
            diag = lax.dot_general(
                q, new_kv(first, TQ, 0), dims, preferred_element_type=jnp.float32
            )
            parts = [(old, cached_kv(0, CACHE, HD)), (diag + diagonal, new_kv(first, TQ, HD))]
            if tile:
                past = lax.dot_general(
                    q, new_kv(0, first, 0), dims, preferred_element_type=jnp.float32
                )
                parts.append((past, new_kv(0, first, HD)))
            row_max = functools.reduce(
                jnp.maximum, [jnp.max(s, -1, keepdims=True) for s, _ in parts]
            )
            shift = row_max * factor
            total, weighted = 0.0, 0.0
            for s, values in parts:
                weights = jnp.exp2(s * factor - shift)
                total = total + jnp.sum(weights, -1, keepdims=True)
                weighted = weighted + jnp.dot(
                    weights.astype(jnp.bfloat16), values, preferred_element_type=jnp.float32
                )
            write(head, first, (weighted / total).astype(jnp.bfloat16))


def attention_kernel(length_ref, qkv_ref, cached_ref, out_ref):
    length = length_ref[0]
    position = lax.broadcasted_iota(jnp.int32, (1, CACHE), 1)
    bias = jnp.where(position < length, 0.0, masked_score)
    rows = lax.broadcasted_iota(jnp.int32, (TQ, TQ), 0)
    cols = lax.broadcasted_iota(jnp.int32, (TQ, TQ), 1)
    diagonal = jnp.where(cols <= rows, 0.0, masked_score)

    def write(head, first, value):
        out_ref[0, first : first + TQ, head * HD : (head + 1) * HD] = value

    head_attention(
        lambda head, first: qkv_ref[0, first : first + TQ, head * HD : (head + 1) * HD],
        lambda first, count, col: qkv_ref[
            0, first : first + count, PER * HD + col : PER * HD + col + HD
        ],
        lambda first, count, col: cached_ref[0, first : first + count, col : col + HD],
        bias,
        diagonal,
        write,
    )


def attention(length, new_qkv, gathered):
    return pl.pallas_call(
        attention_kernel,
        grid=(KVH,),
        out_shape=jax.ShapeDtypeStruct((1, NEW, QH * HD), jnp.bfloat16),
        in_specs=[
            pl.BlockSpec(memory_space=pltpu.SMEM),
            pl.BlockSpec((1, NEW, GROUP), lambda g: (0, 0, g)),
            pl.BlockSpec((1, CACHE, 2 * HD), lambda g: (g, 0, 0)),
        ],
        out_specs=pl.BlockSpec((1, NEW, PER * HD), lambda g: (0, 0, g)),
        cost_estimate=pl.CostEstimate(
            flops=7_500_000_000, bytes_accessed=13_000_000, transcendentals=15_000_000
        ),
        name="attention",
    )(length, new_qkv, gathered)


def route_tables(slot_of, row, n_tok, slot_dev):
    slots = slot_of.reshape(n_tok, slot_dev)
    place = slots % slot_dev
    mine = slots // slot_dev == row
    tok = jnp.arange(n_tok, dtype=jnp.int32)
    eight = jnp.arange(slot_dev, dtype=jnp.int32)
    slot_for_row = jnp.sum(jnp.where(mine, place, 0), 1)
    own = lax.dynamic_slice_in_dim(slots, row, 1)[0] // slot_dev
    request_for_row = jnp.sum(jnp.where(own[None, :] == tok[:, None], eight[None, :], 0), 1)
    hit = mine[:, :, None] & (place[:, :, None] == eight[None, None, :])
    row_of_slot = jnp.sum(jnp.where(hit, tok[:, None, None], 0), (0, 1))
    return slot_for_row, own, request_for_row, row_of_slot


def per_device(new_qkv, kv_cache, lengths, slot_of):
    n_tok = lax.axis_size("tok")
    slot_dev = kv_cache.shape[0]
    row, column = lax.axis_index("tok"), lax.axis_index("head")
    slot_for_row, row_of_request, request_for_row, row_of_slot = route_tables(
        slot_of, row, n_tok, slot_dev
    )
    length = lax.dynamic_slice_in_dim(lengths, row * slot_dev + column, 1)

    sent = jnp.take(kv_cache, slot_for_row, axis=0)
    sent = lax.all_to_all(sent, "tok", split_axis=0, concat_axis=0, tiled=True)
    sent = jnp.take(sent, row_of_request, axis=0)
    gathered = lax.all_to_all(sent, "head", split_axis=0, concat_axis=0, tiled=True)

    fresh = new_qkv.reshape(NEW, KVH, GROUP)[:, :, PER * HD :].transpose(1, 0, 2)
    fresh = lax.all_to_all(fresh, "head", split_axis=0, concat_axis=0, tiled=True)
    fresh = jnp.take(fresh, request_for_row, axis=0)
    fresh = lax.all_to_all(fresh, "tok", split_axis=0, concat_axis=0, tiled=True)
    appended = jnp.take(fresh, row_of_slot, axis=0)
    context = attention(length, new_qkv, gathered)
    return (context, appended)


def solution(mesh):
    return jax.shard_map(
        per_device,
        mesh=mesh,
        in_specs=(P(("tok", "head"), None, None), P("tok", None, "head"), P(), P()),
        out_specs=(P(("tok", "head"), None, None), P("tok", None, "head")),
        check_vma=False,
    )
```

```python
import functools
import math

import jax
import jax.numpy as jnp
from jax import lax
from jax.experimental import pallas as pl
from jax.experimental.pallas import tpu as pltpu
from jax.sharding import PartitionSpec as P

QH = 32
KVH = 8
HD = 128
NEW = 512
CACHE = 512
GROUP = 768
PER = QH // KVH
TQ = 256
MESH = pl.DeviceIdType.MESH

masked_score = -1e30


def head_attention(q_of, new_kv, cached_kv, bias, diagonal, write):
    factor = math.log2(math.e) / math.sqrt(HD)
    dims = (((1,), (1,)), ((), ()))
    for head in range(PER):
        for tile in range(NEW // TQ):
            first = tile * TQ
            q = q_of(head, first)
            old = lax.dot_general(
                q, cached_kv(0, CACHE, 0), dims, preferred_element_type=jnp.float32
            )
            old = old + bias
            diag = lax.dot_general(
                q, new_kv(first, TQ, 0), dims, preferred_element_type=jnp.float32
            )
            parts = [(old, cached_kv(0, CACHE, HD)), (diag + diagonal, new_kv(first, TQ, HD))]
            if tile:
                past = lax.dot_general(
                    q, new_kv(0, first, 0), dims, preferred_element_type=jnp.float32
                )
                parts.append((past, new_kv(0, first, HD)))
            row_max = functools.reduce(
                jnp.maximum, [jnp.max(s, -1, keepdims=True) for s, _ in parts]
            )
            shift = row_max * factor
            total, weighted = 0.0, 0.0
            for s, values in parts:
                weights = jnp.exp2(s * factor - shift)
                total = total + jnp.sum(weights, -1, keepdims=True)
                weighted = weighted + jnp.dot(
                    weights.astype(jnp.bfloat16), values, preferred_element_type=jnp.float32
                )
            write(head, first, (weighted / total).astype(jnp.bfloat16))


def attention_kernel(length_ref, qkv_ref, cached_ref, out_ref):
    length = length_ref[0]
    position = lax.broadcasted_iota(jnp.int32, (1, CACHE), 1)
    bias = jnp.where(position < length, 0.0, masked_score)
    rows = lax.broadcasted_iota(jnp.int32, (TQ, TQ), 0)
    cols = lax.broadcasted_iota(jnp.int32, (TQ, TQ), 1)
    diagonal = jnp.where(cols <= rows, 0.0, masked_score)

    def write(head, first, value):
        out_ref[0, first : first + TQ, head * HD : (head + 1) * HD] = value

    head_attention(
        lambda head, first: qkv_ref[0, first : first + TQ, head * HD : (head + 1) * HD],
        lambda first, count, col: qkv_ref[
            0, first : first + count, PER * HD + col : PER * HD + col + HD
        ],
        lambda first, count, col: cached_ref[0, first : first + count, col : col + HD],
        bias,
        diagonal,
        write,
    )


def attention(length, new_qkv, gathered):
    return pl.pallas_call(
        attention_kernel,
        grid=(KVH,),
        out_shape=jax.ShapeDtypeStruct((1, NEW, QH * HD), jnp.bfloat16),
        in_specs=[
            pl.BlockSpec(memory_space=pltpu.SMEM),
            pl.BlockSpec((1, NEW, GROUP), lambda g: (0, 0, g)),
            pl.BlockSpec((1, CACHE, 2 * HD), lambda g: (g, 0, 0)),
        ],
        out_specs=pl.BlockSpec((1, NEW, PER * HD), lambda g: (0, 0, g)),
        cost_estimate=pl.CostEstimate(
            flops=7_500_000_000, bytes_accessed=13_000_000, transcendentals=15_000_000
        ),
        name="attention",
    )(length, new_qkv, gathered)


def route_tables(slot_of, row, n_tok, slot_dev):
    slots = slot_of.reshape(n_tok, slot_dev)
    place = slots % slot_dev
    mine = slots // slot_dev == row
    tok = jnp.arange(n_tok, dtype=jnp.int32)
    eight = jnp.arange(slot_dev, dtype=jnp.int32)
    slot_for_row = jnp.sum(jnp.where(mine, place, 0), 1)
    own = lax.dynamic_slice_in_dim(slots, row, 1)[0] // slot_dev
    request_for_row = jnp.sum(jnp.where(own[None, :] == tok[:, None], eight[None, :], 0), 1)
    hit = mine[:, :, None] & (place[:, :, None] == eight[None, None, :])
    row_of_slot = jnp.sum(jnp.where(hit, tok[:, None, None], 0), (0, 1))
    return slot_for_row, own, request_for_row, row_of_slot


CHUNKS = 4
PART = NEW // CHUNKS
SUB = 32


def exchange_kernel(
    tables, qkv, cache, gathered, appended, fresh_own, cache_own, *scratch
):
    n_tok, n_head = lax.axis_size("tok"), lax.axis_size("head")
    slot_dev = n_head
    fresh_in, out_old, in_old, to_owner, out_new, in_new = (
        scratch[i * CHUNKS : (i + 1) * CHUNKS] for i in range(6)
    )
    (local, tok_old_s, tok_old_r, tok_new_s, tok_new_r,
     head_old_s, head_old_r, head_new_s, head_new_r) = scratch[6 * CHUNKS :]
    row, column = lax.axis_index("tok"), lax.axis_index("head")
    x, y = row // 4, row % 4

    def tok_peer(k, sign):
        d = (7 * k) % 16
        return ((x + sign * (d // 4) + 4) % 4) * 4 + (y + sign * (d % 4) + 4) % 4

    def head_peer(k, sign):
        return (column + sign * k + n_head) % n_head

    def span(c):
        return pl.ds(c * PART, PART)

    def load_fresh(c, g):
        return pltpu.make_async_copy(
            qkv.at[0, span(c), pl.ds(pl.multiple_of(g * GROUP + PER * HD, 128), 2 * HD)],
            fresh_own.at[g, span(c)],
            local.at[c, g],
        )

    def load_cache(c):
        return pltpu.make_async_copy(
            cache.at[:, span(c)], cache_own.at[:, span(c)], local.at[c, n_head]
        )

    for c in range(CHUNKS):
        load_cache(c).start()
        lax.fori_loop(0, n_head, lambda g, _, c=c: (load_fresh(c, g).start(), 0)[1], 0)

    barrier = pltpu.get_barrier_semaphore()

    def greet_tok(k, _):
        pl.semaphore_signal(
            barrier, inc=1, device_id=(tok_peer(k, 1), column), device_id_type=MESH
        )
        return 0

    def greet_head(k, _):
        pl.semaphore_signal(
            barrier, inc=1, device_id=(row, head_peer(k, 1)), device_id_type=MESH
        )
        return 0

    lax.fori_loop(1, n_tok, greet_tok, 0)
    lax.fori_loop(1, n_head, greet_head, 0)
    pl.semaphore_wait(barrier, n_tok + n_head - 2)

    def tok_send(k, c, out, landing, send, recv):
        to = tok_peer(k, 1)
        return pltpu.make_async_remote_copy(
            src_ref=out[c].at[to],
            dst_ref=landing[c].at[row],
            send_sem=send.at[c, k],
            recv_sem=recv.at[c, k],
            device_id=(to, column),
            device_id_type=MESH,
        )

    def tok_arrival(k, c, out, landing, send, recv):
        return pltpu.make_async_remote_copy(
            src_ref=out[c].at[tok_peer(k, 1)],
            dst_ref=landing[c].at[tok_peer(k, -1)],
            send_sem=send.at[c, k],
            recv_sem=recv.at[c, k],
            device_id=(tok_peer(k, 1), column),
            device_id_type=MESH,
        )

    def head_new(k, c, arrival):
        to = head_peer(k, 1)
        slot = head_peer(k, -1) if arrival else column
        return pltpu.make_async_remote_copy(
            src_ref=fresh_own.at[to, span(c)],
            dst_ref=fresh_in[c].at[slot],
            send_sem=head_new_s.at[c, k],
            recv_sem=head_new_r.at[c, k],
            device_id=(row, to),
            device_id_type=MESH,
        )

    def head_old(k, c, arrival):
        to = head_peer(k, 1)
        slot = head_peer(k, -1) if arrival else column
        return pltpu.make_async_remote_copy(
            src_ref=to_owner[c].at[to],
            dst_ref=gathered.at[slot, span(c)],
            send_sem=head_old_s.at[c, k],
            recv_sem=head_old_r.at[c, k],
            device_id=(row, to),
            device_id_type=MESH,
        )

    def each(first, count, fn):
        lax.fori_loop(first, count, lambda k, _: (fn(k), 0)[1], 0)

    def move(count, source, base, index_of, store):
        def one(i):
            picked = index_of(i)
            for s in range(0, PART, SUB):
                store(i, s, source[picked, base + s : base + s + SUB, :])

        each(0, count, one)

    old = (out_old, in_old, tok_old_s, tok_old_r)
    new = (out_new, in_new, tok_new_s, tok_new_r)

    def start_fresh(c):
        each(0, n_head, lambda g: load_fresh(c, g).wait())
        each(1, n_head, lambda k: head_new(k, c, False).start())
        fresh_in[c][column] = fresh_own[column, span(c), :]

    def into(ref):
        def store(i, s, value):
            ref[i, s : s + SUB, :] = value

        return store

    def start_old(c):
        move(n_tok, cache_own, c * PART, lambda i: tables[i], into(out_old[c]))
        each(1, n_tok, lambda k: tok_send(k, c, *old).start())
        in_old[c][row] = out_old[c][row]

    def relay_new(c):
        each(1, n_head, lambda k: head_new(k, c, True).wait_recv())
        move(n_tok, fresh_in[c], 0, lambda i: tables[24 + i], into(out_new[c]))
        each(1, n_tok, lambda k: tok_send(k, c, *new).start())
        in_new[c][row] = out_new[c][row]

    def relay_old(c):
        each(1, n_tok, lambda k: tok_arrival(k, c, *old).wait_recv())
        move(n_head, in_old[c], 0, lambda i: tables[16 + i], into(to_owner[c]))
        each(1, n_head, lambda k: head_old(k, c, False).start())
        gathered[column, span(c), :] = to_owner[c][column]

    def finish_new(c):
        def store(i, s, value):
            appended[i, c * PART + s : c * PART + s + SUB, :] = value

        each(1, n_tok, lambda k: tok_arrival(k, c, *new).wait_recv())
        move(slot_dev, in_new[c], 0, lambda i: tables[40 + i], store)

    for c in range(CHUNKS):
        load_cache(c).wait()
    for c in range(CHUNKS):
        start_fresh(c)
        start_old(c)
    for c in range(CHUNKS):
        relay_new(c)
        relay_old(c)
    for c in range(CHUNKS):
        finish_new(c)
    for c in range(CHUNKS):
        each(1, n_head, lambda k, c=c: head_old(k, c, True).wait_recv())
    for c in range(CHUNKS):
        each(1, n_head, lambda k, c=c: head_new(k, c, False).wait_send())
        each(1, n_head, lambda k, c=c: head_old(k, c, False).wait_send())
        each(1, n_tok, lambda k, c=c: tok_send(k, c, *old).wait_send())
        each(1, n_tok, lambda k, c=c: tok_send(k, c, *new).wait_send())


def exchange(tables, new_qkv, kv_cache, n_tok, n_head):
    block = jax.ShapeDtypeStruct(kv_cache.shape, kv_cache.dtype)
    bf16 = jnp.bfloat16
    dma = pltpu.SemaphoreType.DMA
    scratch = [pltpu.VMEM((n_head, NEW, 2 * HD), bf16)] * 2
    for count in (n_head, n_tok, n_tok, n_head, n_tok, n_tok):
        scratch += [pltpu.VMEM((count, PART, 2 * HD), bf16)] * CHUNKS
    scratch += [dma((CHUNKS, n_head + 1))]
    scratch += [dma((CHUNKS, n_tok))] * 4 + [dma((CHUNKS, n_head))] * 4
    return pl.pallas_call(
        exchange_kernel,
        out_shape=(block, block),
        in_specs=[
            pl.BlockSpec(memory_space=pltpu.SMEM),
            pl.BlockSpec(memory_space=pl.ANY),
            pl.BlockSpec(memory_space=pl.ANY),
        ],
        out_specs=[pl.BlockSpec(memory_space=pltpu.VMEM)] * 2,
        scratch_shapes=scratch,
        compiler_params=pltpu.CompilerParams(
            collective_id=0, has_side_effects=True, vmem_limit_bytes=56 << 20
        ),
        name="exchange",
    )(tables, new_qkv, kv_cache)


def per_device(new_qkv, kv_cache, lengths, slot_of):
    n_tok, n_head = lax.axis_size("tok"), lax.axis_size("head")
    slot_dev = kv_cache.shape[0]
    row, column = lax.axis_index("tok"), lax.axis_index("head")
    slot_for_row, row_of_request, request_for_row, row_of_slot = route_tables(
        slot_of, row, n_tok, slot_dev
    )
    tables = jnp.concatenate([slot_for_row, row_of_request, request_for_row, row_of_slot])
    length = lax.dynamic_slice_in_dim(lengths, row * slot_dev + column, 1)
    gathered, appended = exchange(tables, new_qkv, kv_cache, n_tok, n_head)
    context = attention(length, new_qkv, gathered)
    return (context, appended)


def solution(mesh):
    return jax.shard_map(
        per_device,
        mesh=mesh,
        in_specs=(P(("tok", "head"), None, None), P("tok", None, "head"), P(), P()),
        out_specs=(P(("tok", "head"), None, None), P("tok", None, "head")),
        check_vma=False,
    )
```

```python
import functools
import math

import jax
import jax.numpy as jnp
from jax import lax
from jax.experimental import pallas as pl
from jax.experimental.pallas import tpu as pltpu
from jax.sharding import PartitionSpec as P

QH = 32
KVH = 8
HD = 128
NEW = 512
CACHE = 512
GROUP = 768
PER = QH // KVH
TQ = 256
MESH = pl.DeviceIdType.MESH

masked_score = -1e30


def head_attention(q_of, new_kv, cached_kv, bias, diagonal, write):
    factor = math.log2(math.e) / math.sqrt(HD)
    dims = (((1,), (1,)), ((), ()))
    for head in range(PER):
        for tile in range(NEW // TQ):
            first = tile * TQ
            q = q_of(head, first)
            old = lax.dot_general(
                q, cached_kv(0, CACHE, 0), dims, preferred_element_type=jnp.float32
            )
            old = old + bias
            diag = lax.dot_general(
                q, new_kv(first, TQ, 0), dims, preferred_element_type=jnp.float32
            )
            parts = [(old, cached_kv(0, CACHE, HD)), (diag + diagonal, new_kv(first, TQ, HD))]
            if tile:
                past = lax.dot_general(
                    q, new_kv(0, first, 0), dims, preferred_element_type=jnp.float32
                )
                parts.append((past, new_kv(0, first, HD)))
            row_max = functools.reduce(
                jnp.maximum, [jnp.max(s, -1, keepdims=True) for s, _ in parts]
            )
            shift = row_max * factor
            total, weighted = 0.0, 0.0
            for s, values in parts:
                weights = jnp.exp2(s * factor - shift)
                total = total + jnp.sum(weights, -1, keepdims=True)
                weighted = weighted + jnp.dot(
                    weights.astype(jnp.bfloat16), values, preferred_element_type=jnp.float32
                )
            write(head, first, (weighted / total).astype(jnp.bfloat16))


def masks(length):
    position = lax.broadcasted_iota(jnp.int32, (1, CACHE), 1)
    bias = jnp.where(position < length, 0.0, masked_score)
    rows = lax.broadcasted_iota(jnp.int32, (TQ, TQ), 0)
    cols = lax.broadcasted_iota(jnp.int32, (TQ, TQ), 1)
    return bias, jnp.where(cols <= rows, 0.0, masked_score)


def route_tables(slot_of, row, n_tok, slot_dev):
    slots = slot_of.reshape(n_tok, slot_dev)
    place = slots % slot_dev
    mine = slots // slot_dev == row
    tok = jnp.arange(n_tok, dtype=jnp.int32)
    eight = jnp.arange(slot_dev, dtype=jnp.int32)
    slot_for_row = jnp.sum(jnp.where(mine, place, 0), 1)
    own = lax.dynamic_slice_in_dim(slots, row, 1)[0] // slot_dev
    request_for_row = jnp.sum(jnp.where(own[None, :] == tok[:, None], eight[None, :], 0), 1)
    hit = mine[:, :, None] & (place[:, :, None] == eight[None, None, :])
    row_of_slot = jnp.sum(jnp.where(hit, tok[:, None, None], 0), (0, 1))
    return slot_for_row, own, request_for_row, row_of_slot


CHUNKS = 4
PART = NEW // CHUNKS
SUB = 32


def exchange_kernel(
    tables, qkv, cache, context, appended, qkv_own, cache_own, gathered, context_own, *scratch
):
    n_tok, n_head = lax.axis_size("tok"), lax.axis_size("head")
    slot_dev = n_head
    fresh_in, out_old, in_old, to_owner, out_new, in_new = (
        scratch[i * CHUNKS : (i + 1) * CHUNKS] for i in range(6)
    )
    (local, tok_old_s, tok_old_r, tok_new_s, tok_new_r,
     head_old_s, head_old_r, head_new_s, head_new_r, written) = scratch[6 * CHUNKS :]
    row, column = lax.axis_index("tok"), lax.axis_index("head")
    x, y = row // 4, row % 4

    def tok_peer(k, sign):
        d = (7 * k) % 16
        return ((x + sign * (d // 4) + 4) % 4) * 4 + (y + sign * (d % 4) + 4) % 4

    def head_peer(k, sign):
        return (column + sign * k + n_head) % n_head

    def span(c):
        return pl.ds(c * PART, PART)

    def load_fresh(c, g):
        return pltpu.make_async_copy(
            qkv.at[0, span(c), pl.ds(pl.multiple_of(g * GROUP, 128), GROUP)],
            qkv_own.at[g, span(c)],
            local.at[c, g],
        )

    def load_cache(c):
        return pltpu.make_async_copy(
            cache.at[:, span(c)], cache_own.at[:, span(c)], local.at[c, n_head]
        )

    for c in range(CHUNKS):
        load_cache(c).start()
        lax.fori_loop(0, n_head, lambda g, _, c=c: (load_fresh(c, g).start(), 0)[1], 0)

    barrier = pltpu.get_barrier_semaphore()

    def greet_tok(k, _):
        pl.semaphore_signal(
            barrier, inc=1, device_id=(tok_peer(k, 1), column), device_id_type=MESH
        )
        return 0

    def greet_head(k, _):
        pl.semaphore_signal(
            barrier, inc=1, device_id=(row, head_peer(k, 1)), device_id_type=MESH
        )
        return 0

    lax.fori_loop(1, n_tok, greet_tok, 0)
    lax.fori_loop(1, n_head, greet_head, 0)
    pl.semaphore_wait(barrier, n_tok + n_head - 2)

    def tok_send(k, c, out, landing, send, recv):
        to = tok_peer(k, 1)
        return pltpu.make_async_remote_copy(
            src_ref=out[c].at[to],
            dst_ref=landing[c].at[row],
            send_sem=send.at[c, k],
            recv_sem=recv.at[c, k],
            device_id=(to, column),
            device_id_type=MESH,
        )

    def tok_arrival(k, c, out, landing, send, recv):
        return pltpu.make_async_remote_copy(
            src_ref=out[c].at[tok_peer(k, 1)],
            dst_ref=landing[c].at[tok_peer(k, -1)],
            send_sem=send.at[c, k],
            recv_sem=recv.at[c, k],
            device_id=(tok_peer(k, 1), column),
            device_id_type=MESH,
        )

    def head_new(k, c, arrival):
        to = head_peer(k, 1)
        slot = head_peer(k, -1) if arrival else column
        return pltpu.make_async_remote_copy(
            src_ref=qkv_own.at[to, span(c), pl.ds(PER * HD, 2 * HD)],
            dst_ref=fresh_in[c].at[slot],
            send_sem=head_new_s.at[c, k],
            recv_sem=head_new_r.at[c, k],
            device_id=(row, to),
            device_id_type=MESH,
        )

    def head_old(k, c, arrival):
        to = head_peer(k, 1)
        slot = head_peer(k, -1) if arrival else column
        return pltpu.make_async_remote_copy(
            src_ref=to_owner[c].at[to],
            dst_ref=gathered.at[slot, span(c)],
            send_sem=head_old_s.at[c, k],
            recv_sem=head_old_r.at[c, k],
            device_id=(row, to),
            device_id_type=MESH,
        )

    def each(first, count, fn):
        lax.fori_loop(first, count, lambda k, _: (fn(k), 0)[1], 0)

    def move(count, source, base, index_of, store):
        def one(i):
            picked = index_of(i)
            for s in range(0, PART, SUB):
                store(i, s, source[picked, base + s : base + s + SUB, :])

        each(0, count, one)

    old = (out_old, in_old, tok_old_s, tok_old_r)
    new = (out_new, in_new, tok_new_s, tok_new_r)

    def start_fresh(c):
        each(0, n_head, lambda g: load_fresh(c, g).wait())
        each(1, n_head, lambda k: head_new(k, c, False).start())
        fresh_in[c][column] = qkv_own[column, span(c), PER * HD :]

    def into(ref):
        def store(i, s, value):
            ref[i, s : s + SUB, :] = value

        return store

    def start_old(c):
        move(n_tok, cache_own, c * PART, lambda i: tables[i], into(out_old[c]))
        each(1, n_tok, lambda k: tok_send(k, c, *old).start())
        in_old[c][row] = out_old[c][row]

    def relay_new(c):
        each(1, n_head, lambda k: head_new(k, c, True).wait_recv())
        move(n_tok, fresh_in[c], 0, lambda i: tables[24 + i], into(out_new[c]))
        each(1, n_tok, lambda k: tok_send(k, c, *new).start())
        in_new[c][row] = out_new[c][row]

    def relay_old(c):
        each(1, n_tok, lambda k: tok_arrival(k, c, *old).wait_recv())
        move(n_head, in_old[c], 0, lambda i: tables[16 + i], into(to_owner[c]))
        each(1, n_head, lambda k: head_old(k, c, False).start())
        gathered[column, span(c), :] = to_owner[c][column]

    def finish_new(c):
        def store(i, s, value):
            appended[i, c * PART + s : c * PART + s + SUB, :] = value

        each(1, n_tok, lambda k: tok_arrival(k, c, *new).wait_recv())
        move(slot_dev, in_new[c], 0, lambda i: tables[40 + i], store)

    for c in range(CHUNKS):
        load_cache(c).wait()
    for c in range(CHUNKS):
        start_fresh(c)
        start_old(c)
    for c in range(CHUNKS):
        relay_new(c)
    for c in range(CHUNKS):
        relay_old(c)
    for c in range(CHUNKS):
        each(1, n_head, lambda k, c=c: head_old(k, c, True).wait_recv())

    bias, diagonal = masks(tables[48])

    def write_out(g):
        return pltpu.make_async_copy(
            context_own.at[g],
            context.at[0, :, pl.ds(pl.multiple_of(g * PER * HD, 128), PER * HD)],
            written.at[g],
        )

    def attend(g):
        def write(head, first, value):
            context_own[g, first : first + TQ, head * HD : (head + 1) * HD] = value

        head_attention(
            lambda head, first: qkv_own[
                g, first : first + TQ, head * HD : (head + 1) * HD
            ],
            lambda first, count, col: qkv_own[
                g, first : first + count, PER * HD + col : PER * HD + col + HD
            ],
            lambda first, count, col: gathered[g, first : first + count, col : col + HD],
            bias,
            diagonal,
            write,
        )
        write_out(g).start()

    each(0, n_head, attend)
    for c in range(CHUNKS):
        finish_new(c)
    each(0, n_head, lambda g: write_out(g).wait())
    for c in range(CHUNKS):
        each(1, n_head, lambda k, c=c: head_new(k, c, False).wait_send())
        each(1, n_head, lambda k, c=c: head_old(k, c, False).wait_send())
        each(1, n_tok, lambda k, c=c: tok_send(k, c, *old).wait_send())
        each(1, n_tok, lambda k, c=c: tok_send(k, c, *new).wait_send())


def exchange(tables, new_qkv, kv_cache, n_tok, n_head):
    bf16 = jnp.bfloat16
    results = (
        jax.ShapeDtypeStruct((1, NEW, QH * HD), bf16),
        jax.ShapeDtypeStruct(kv_cache.shape, bf16),
    )
    dma = pltpu.SemaphoreType.DMA
    scratch = [
        pltpu.VMEM((n_head, NEW, width), bf16) for width in (GROUP, 2 * HD, 2 * HD, PER * HD)
    ]
    for count in (n_head, n_tok, n_tok, n_head, n_tok, n_tok):
        scratch += [pltpu.VMEM((count, PART, 2 * HD), bf16)] * CHUNKS
    scratch += [dma((CHUNKS, n_head + 1))]
    scratch += [dma((CHUNKS, n_tok))] * 4 + [dma((CHUNKS, n_head))] * 4 + [dma((n_head,))]
    return pl.pallas_call(
        exchange_kernel,
        out_shape=results,
        in_specs=[
            pl.BlockSpec(memory_space=pltpu.SMEM),
            pl.BlockSpec(memory_space=pl.ANY),
            pl.BlockSpec(memory_space=pl.ANY),
        ],
        out_specs=[
            pl.BlockSpec(memory_space=pl.ANY),
            pl.BlockSpec(memory_space=pltpu.VMEM),
        ],
        scratch_shapes=scratch,
        compiler_params=pltpu.CompilerParams(
            collective_id=0, has_side_effects=True, vmem_limit_bytes=56 << 20
        ),
        name="exchange",
    )(tables, new_qkv, kv_cache)


def per_device(new_qkv, kv_cache, lengths, slot_of):
    n_tok, n_head = lax.axis_size("tok"), lax.axis_size("head")
    slot_dev = kv_cache.shape[0]
    row, column = lax.axis_index("tok"), lax.axis_index("head")
    slot_for_row, row_of_request, request_for_row, row_of_slot = route_tables(
        slot_of, row, n_tok, slot_dev
    )
    length = lax.dynamic_slice_in_dim(lengths, row * slot_dev + column, 1)
    tables = jnp.concatenate(
        [slot_for_row, row_of_request, request_for_row, row_of_slot, length]
    )
    return exchange(tables, new_qkv, kv_cache, n_tok, n_head)


def solution(mesh):
    return jax.shard_map(
        per_device,
        mesh=mesh,
        in_specs=(P(("tok", "head"), None, None), P("tok", None, "head"), P(), P()),
        out_specs=(P(("tok", "head"), None, None), P("tok", None, "head")),
        check_vma=False,
    )
```
